32 devices in a mesh: dp: 8 (over z, x), mp: 4 (over y, core).
Axes of the slice: x: 2, y: 2, z: 4, core: 2. Of those that a mesh axis runs over, the one named last changes fastest.
Arguments:
- features: bfloat16 [8192, 1024], P('dp'), may hold values from -6 to 6
- out_grads: bfloat16 [8192, 4, 1024], P('dp', None, 'mp'), may hold values from -0.0625 to 0.0625
- norm_grads: float32 [8, 2048], P('dp'), may hold values from -2 to 2
- owners: int32 [5], replicated, may hold values from 0 to 7, as said below
- moment1: float32 [4, 1024, 1024], P(None, 'dp', 'mp'), may hold values from -6 to 6
- moment2: float32 [4, 1024, 1024], P(None, 'dp', 'mp'), may hold values from 0.1 to 10
- left_stats: float32 [4, 1024, 1024], P(None, 'dp', 'mp'), may hold values from -1024 to 1024, as said below
- right_stats: float32 [4, 1024, 1024], P(None, 'dp', 'mp'), may hold values from -1024 to 1024, as said below
- left_basis: float32 [4, 1024, 1024], P(None, 'dp', 'mp'), may hold values from -1 to 2
- right_basis: float32 [4, 1024, 1024], P(None, 'dp', 'mp'), may hold values from -1 to 2
- norm_m: float32 [2048], P('dp'), may hold values from -6 to 6
- norm_v: float32 [2048], P('dp'), may hold values from 0.1 to 10
Outputs:
- new_moment1: float32 [4, 1024, 1024], P(None, 'dp', 'mp')
- new_moment2: float32 [4, 1024, 1024], P(None, 'dp', 'mp')
- new_left_stats: float32 [4, 1024, 1024], P(None, 'dp', 'mp')
- new_right_stats: float32 [4, 1024, 1024], P(None, 'dp', 'mp')
- new_left_basis: float32 [4, 1024, 1024], P(None, 'dp', 'mp')
- new_right_basis: float32 [4, 1024, 1024], P(None, 'dp', 'mp')
- update_slots: bfloat16 [8, 1024, 1024], P('dp', None, 'mp')
- new_norm_m: float32 [2048], P('dp')
- new_norm_v: float32 [2048], P('dp')
- norm_slots: float32 [8, 2048], P('dp')
The draws below stay inside these ranges and needn't reach their ends.
Inputs may be any that keep to these rules, and one draw needn't show every extreme that they name: `owners`: the first 4 entries are distinct, so a dp index owns at most one tile; the last entry may equal any of them. `left_stats`: each tile of statistics is symmetric. `right_stats`: each tile of statistics is symmetric.
All inputs are finite; a program needn't handle non-finite values.
Results may differ from the reference program's by a relative error of at most 0.0072.
Values may be sent and summed in bfloat16 or wider, within the bound.
A program may use at most 128 MiB of HBM per device.

```python
import math
import jax
import jax.numpy as jnp
from jax import lax

D = 2048
TILE = 1024
NT = 4
TOKENS = 8192
N_DP = 8


def stats_single(key):
    key_diag, key_noise = jax.random.split(key)
    diag = TILE * jnp.exp(jax.random.uniform(key_diag, (TILE,), jnp.float32, math.log(0.1), 0.0))
    noise = jax.random.normal(key_noise, (TILE, TILE), jnp.float32)
    symmetric = (noise + noise.T) * 0.70710678
    scale = jnp.sqrt(diag[:, None] * diag[None, :]) * (0.3 / math.sqrt(TILE))
    positions = jnp.arange(TILE, dtype=jnp.int32)
    on_diag = positions[:, None] == positions[None, :]
    return jnp.where(on_diag, diag[:, None], scale * symmetric)


def basis_single(key):
    noise = jax.random.normal(key, (TILE, TILE), jnp.float32)
    positions = jnp.arange(TILE, dtype=jnp.int32)
    on_diag = (positions[:, None] == positions[None, :]).astype(jnp.float32)
    return on_diag + noise * (0.3 / math.sqrt(TILE))


def draw_owners(key, part):
    key_perm, key_mix, key_norm = jax.random.split(jax.random.fold_in(key, 5), 3)
    middle = (1 + jax.random.permutation(key_perm, N_DP - 2)[:NT - 2]).astype(jnp.int32)
    ends = jnp.array([0, N_DP - 1], dtype=jnp.int32)
    tiles = jax.random.permutation(key_mix, jnp.concatenate([ends, middle])).astype(jnp.int32)
    norm_owner = jax.random.randint(key_norm, (1,), 0, N_DP).astype(jnp.int32)
    return jnp.concatenate([tiles, norm_owner]).astype(jnp.int32)


def draw_left_stats(key, part):
    return jax.vmap(stats_single)(jax.random.split(jax.random.fold_in(key, 11), NT))


def draw_right_stats(key, part):
    return jax.vmap(stats_single)(jax.random.split(jax.random.fold_in(key, 13), NT))


def draw_left_basis(key, part):
    return jax.vmap(basis_single)(jax.random.split(jax.random.fold_in(key, 17), NT))


def draw_right_basis(key, part):
    return jax.vmap(basis_single)(jax.random.split(jax.random.fold_in(key, 19), NT))


def block_levels(stream_key, shape, cuts, low, top_value):
    gain = 1.0
    for dim, shards_of in cuts:
        heights = jax.random.uniform(jax.random.fold_in(jax.random.fold_in(stream_key, 6), dim), (shards_of,), jnp.float32, low / len(cuts), top_value / len(cuts))
        gain = gain * jnp.repeat(jnp.exp(heights), shape[dim] // shards_of).reshape((-1,) + (1,) * (len(shape) - 1 - dim))
    return gain


def gaussian(key, extent, scale, reach, pieces=(), kind=jnp.bfloat16):
    gain = block_levels(key, extent, pieces, -0.22, 0.18) if pieces else 1.0
    values = jax.random.normal(key, extent, jnp.float32) * scale * gain
    return jnp.minimum(jnp.maximum(values, -reach), reach).astype(kind)


def setup_inputs(seed: int = 0) -> dict:
    streams_of = jax.random.split(jax.random.key(seed), 13)
    return {
        "features": gaussian(streams_of[0], (TOKENS, TILE), 1.0, 6.0, ((0, 8),)),
        "out_grads": gaussian(streams_of[1], (TOKENS, NT, TILE), TOKENS ** -0.5, 0.0625, ((0, 8), (2, 4))),
        "norm_grads": gaussian(streams_of[2], (N_DP, D), N_DP ** -0.5, 2.0, ((0, 8),), jnp.float32),
        "owners": draw_owners(jax.random.fold_in(streams_of[12], 71), 0),
        "moment1": gaussian(streams_of[4], (NT, TILE, TILE), 1.0, 6.0, ((1, 8), (2, 4)), jnp.float32),
        "moment2": jnp.clip(jnp.exp(math.log(10.0) - 4.6051702 * jax.random.uniform(streams_of[5], (NT, TILE, TILE), jnp.float32) ** block_levels(streams_of[5], (NT, TILE, TILE), ((1, 8), (2, 4)), -0.2, 0.2)), 0.1, 10.0),
        "left_stats": draw_left_stats(jax.random.fold_in(streams_of[12], 71), 0),
        "right_stats": draw_right_stats(jax.random.fold_in(streams_of[12], 71), 0),
        "left_basis": draw_left_basis(jax.random.fold_in(streams_of[12], 71), 0),
        "right_basis": draw_right_basis(jax.random.fold_in(streams_of[12], 71), 0),
        "norm_m": gaussian(streams_of[10], (D,), 1.0, 6.0, ((0, 8),), jnp.float32),
        "norm_v": jnp.clip(jnp.exp(math.log(10.0) - 4.6051702 * jax.random.uniform(streams_of[11], (D,), jnp.float32) ** block_levels(streams_of[11], (D,), ((0, 8),), -0.2, 0.2)), 0.1, 10.0),
    }


FIX_ONE = 1.0 - 0.9 ** 10
FIX_TWO = 1.0 - 0.95 ** 10

def contract(left, right, left_dim, right_dim):
    return lax.dot_general(left, right, (((left_dim,), (right_dim,)), ((), ())), preferred_element_type=jnp.float32)

def reference(features, out_grads, norm_grads, owners, moment1, moment2, left_stats, right_stats, left_basis, right_basis, norm_m, norm_v):

    def tile_step(items):
        index, mom_one, mom_two, stats_l, stats_r, basis_l, basis_r = items
        grad_cols = lax.dynamic_index_in_dim(out_grads, index, 1, keepdims=False)
        grad = contract(features, grad_cols, 0, 0)
        grad_b = grad.astype(jnp.bfloat16)
        left_b = basis_l.astype(jnp.bfloat16)
        right_b = basis_r.astype(jnp.bfloat16)
        inner = jnp.dot(grad_b, right_b, preferred_element_type=jnp.float32).astype(jnp.bfloat16)
        rotated = contract(left_b, inner, 0, 0)
        new_one = 0.9 * mom_one + 0.1 * rotated
        new_two = 0.95 * mom_two + 0.05 * rotated * rotated
        direction = (new_one / FIX_ONE / (jnp.sqrt(new_two / FIX_TWO) + 1e-08)).astype(jnp.bfloat16)
        back = contract(direction, right_b, 1, 1).astype(jnp.bfloat16)
        update = jnp.dot(left_b, back, preferred_element_type=jnp.float32).astype(jnp.bfloat16)
        new_sl = 0.95 * stats_l + 0.05 * contract(grad_b, grad_b, 1, 1)
        new_sr = 0.95 * stats_r + 0.05 * contract(grad_b, grad_b, 0, 0)
        power_l = jnp.dot(new_sl.astype(jnp.bfloat16), left_b, preferred_element_type=jnp.float32)
        power_r = jnp.dot(new_sr.astype(jnp.bfloat16), right_b, preferred_element_type=jnp.float32)
        iter_l = (power_l * lax.rsqrt(lax.optimization_barrier(jnp.sum(power_l * power_l, axis=0, keepdims=True)) + 1e-06)).astype(jnp.bfloat16)
        iter_r = (power_r * lax.rsqrt(lax.optimization_barrier(jnp.sum(power_r * power_r, axis=0, keepdims=True)) + 1e-06)).astype(jnp.bfloat16)
        gram_l = contract(iter_l, iter_l, 0, 0).astype(jnp.bfloat16)
        gram_r = contract(iter_r, iter_r, 0, 0).astype(jnp.bfloat16)
        new_bl = 1.5 * iter_l.astype(jnp.float32) - 0.5 * jnp.dot(iter_l, gram_l, preferred_element_type=jnp.float32)
        new_br = 1.5 * iter_r.astype(jnp.float32) - 0.5 * jnp.dot(iter_r, gram_r, preferred_element_type=jnp.float32)
        return (new_one, new_two, new_sl, new_sr, new_bl, new_br, update)
    indices = jnp.arange(NT, dtype=jnp.int32)
    results = lax.map(tile_step, (indices, moment1, moment2, left_stats, right_stats, left_basis, right_basis))
    new_one, new_two, new_sl, new_sr, new_bl, new_br, updates = results
    update_slots = jnp.zeros((N_DP, TILE, TILE), jnp.bfloat16).at[owners[:NT]].set(updates)
    norm_total = lax.optimization_barrier(jnp.sum(norm_grads, axis=0))
    new_nm = 0.9 * norm_m + 0.1 * norm_total
    new_nv = 0.95 * norm_v + 0.05 * norm_total * norm_total
    norm_step = new_nm / FIX_ONE / (jnp.sqrt(new_nv / FIX_TWO) + 1e-08)
    norm_slots = jnp.zeros((N_DP, D), jnp.float32).at[owners[NT]].set(norm_step)
    return (new_one, new_two, new_sl, new_sr, new_bl, new_br, update_slots, new_nm, new_nv, norm_slots)
```

```python
import jax
import jax.numpy as jnp
from jax import lax
from jax.sharding import PartitionSpec as P

FIX_ONE = 1.0 - 0.9**10
FIX_TWO = 1.0 - 0.95**10
BF = jnp.bfloat16
F32 = jnp.float32


def contract(left, right, left_dim, right_dim):
    return lax.dot_general(
        left, right, (((left_dim,), (right_dim,)), ((), ())), preferred_element_type=F32
    )


def to_tile(blocks):
    out = lax.all_to_all(blocks, "mp", split_axis=1, concat_axis=1, tiled=True)
    k, n, r, c = out.shape
    return out.transpose(0, 2, 1, 3).reshape(k, r, n * c)


def to_home(rows, n):
    k, r, c = rows.shape
    out = rows.reshape(k, r, n, c // n).transpose(0, 2, 1, 3)
    return lax.all_to_all(out, "mp", split_axis=1, concat_axis=1, tiled=True)


def gather_rows(rows):
    return lax.all_gather(rows, "dp", axis=0, tiled=True)


def normalize(power):
    wide = power.astype(F32)
    return lax.rsqrt(jnp.sum(wide * wide, axis=0, keepdims=True) + 1e-06)


def shards(
    features,
    out_grads,
    norm_grads,
    owners,
    moment1,
    moment2,
    left_stats,
    right_stats,
    left_basis,
    right_basis,
    norm_m,
    norm_v,
):
    dp = lax.axis_size("dp")
    tiles, slab, width = moment1.shape
    full = slab * dp
    me = lax.axis_index("dp")
    row0 = me * slab

    narrow = to_tile(jnp.stack([left_basis, right_basis, left_stats, right_stats]).astype(BF))
    left_full = gather_rows(narrow[0])
    right_full = gather_rows(narrow[1])

    flat = out_grads.reshape(out_grads.shape[0], tiles * width)
    partial = contract(features, flat, 0, 0).astype(BF).reshape(dp, slab, tiles * width)
    parts = lax.all_to_all(partial, "dp", split_axis=0, concat_axis=0, tiled=True)
    grad_home = jnp.sum(parts.astype(F32), axis=0).astype(BF)
    grad_home = grad_home.reshape(slab, tiles, width).transpose(1, 0, 2)
    grad_rows = to_tile(grad_home[None])[0]
    grad_full = gather_rows(grad_rows)

    wide = to_tile(jnp.stack([moment1, moment2]))

    prod_l = contract(grad_rows, grad_full, 1, 1)
    grad_cols = lax.dynamic_slice_in_dim(grad_full, row0, slab, 1)
    prod_r = contract(grad_cols, grad_full, 0, 0)
    stats_l = (0.95 * narrow[2].astype(F32) + 0.05 * prod_l).astype(BF)
    stats_r = (0.95 * narrow[3].astype(F32) + 0.05 * prod_r).astype(BF)
    power_l = contract(stats_l, left_full, 1, 0).astype(BF)
    power_r = contract(stats_r, right_full, 1, 0).astype(BF)
    power_l_full = gather_rows(power_l)
    power_r_full = gather_rows(power_r)

    left_cols = lax.dynamic_slice_in_dim(left_full, row0, slab, 1)
    half = contract(left_cols, grad_full, 0, 0).astype(BF)
    rotated = contract(half, right_full, 1, 0)
    tile_one = 0.9 * wide[0] + 0.1 * rotated
    tile_two = 0.95 * wide[1] + 0.05 * rotated * rotated
    direction = (tile_one / FIX_ONE / (jnp.sqrt(tile_two / FIX_TWO) + 1e-08)).astype(BF)
    back = contract(direction, right_full, 1, 1).astype(BF)
    back_full = gather_rows(back)

    home1 = to_home(jnp.stack([rotated, prod_l, prod_r]).astype(BF), tiles).astype(F32)
    new_one = 0.9 * moment1 + 0.1 * home1[0]
    new_two = 0.95 * moment2 + 0.05 * home1[0] * home1[0]
    new_sl = 0.95 * left_stats + 0.05 * home1[1]
    new_sr = 0.95 * right_stats + 0.05 * home1[2]

    update = contract(narrow[0], back_full, 1, 0).astype(BF)

    def refine(power_full, power_rows):
        scale = normalize(power_full)
        iter_full = (power_full.astype(F32) * scale).astype(BF)
        iter_rows = (power_rows.astype(F32) * scale).astype(BF)
        gram = contract(iter_rows, iter_full, 1, 1).astype(BF)
        return 1.5 * iter_rows.astype(F32) - 0.5 * contract(gram, iter_full, 1, 0)

    new_l = refine(power_l_full, power_l)
    new_r = refine(power_r_full, power_r)
    home2 = to_home(jnp.stack([new_l.astype(BF), new_r.astype(BF), update]), tiles)
    new_bl = home2[0].astype(F32)
    new_br = home2[1].astype(F32)
    slot_of = jnp.arange(dp, dtype=jnp.int32)[:, None, None]
    slots = jnp.zeros((dp, slab, width), BF)
    for n in range(tiles):
        slots = jnp.where(slot_of == owners[n], home2[2, n][None], slots)
    update_slot = lax.all_to_all(slots, "dp", split_axis=0, concat_axis=0, tiled=True)
    update_slot = update_slot.reshape(1, full, width)

    packed = jnp.concatenate([norm_grads[0], norm_m, norm_v])[None]
    everyone = lax.all_gather(packed, "dp", axis=0, tiled=True)
    size = norm_grads.shape[1]
    part = norm_m.shape[0]
    norm_total = jnp.sum(everyone[:, :size], axis=0)
    all_nm = 0.9 * everyone[:, size : size + part].reshape(size) + 0.1 * norm_total
    all_nv = (
        0.95 * everyone[:, size + part :].reshape(size) + 0.05 * norm_total * norm_total
    )
    norm_step = all_nm / FIX_ONE / (jnp.sqrt(all_nv / FIX_TWO) + 1e-08)
    norm_slot = jnp.where(me == owners[tiles], norm_step, 0.0)[None]
    new_nm = lax.dynamic_slice_in_dim(all_nm, me * part, part, 0)
    new_nv = lax.dynamic_slice_in_dim(all_nv, me * part, part, 0)
    return (
        new_one,
        new_two,
        new_sl,
        new_sr,
        new_bl,
        new_br,
        update_slot,
        new_nm,
        new_nv,
        norm_slot,
    )


def solution(mesh):
    in_specs = (
        P("dp", None),
        P("dp", None, "mp"),
        P("dp", None),
        P(),
        P(None, "dp", "mp"),
        P(None, "dp", "mp"),
        P(None, "dp", "mp"),
        P(None, "dp", "mp"),
        P(None, "dp", "mp"),
        P(None, "dp", "mp"),
        P("dp"),
        P("dp"),
    )
    out_specs = (
        P(None, "dp", "mp"),
        P(None, "dp", "mp"),
        P(None, "dp", "mp"),
        P(None, "dp", "mp"),
        P(None, "dp", "mp"),
        P(None, "dp", "mp"),
        P("dp", None, "mp"),
        P("dp"),
        P("dp"),
        P("dp", None),
    )
    return jax.shard_map(shards, mesh=mesh, in_specs=in_specs, out_specs=out_specs, check_vma=False)
```

```python
import jax
import jax.numpy as jnp
from jax import lax
from jax.sharding import PartitionSpec as P

FIX_ONE = 1.0 - 0.9**10
FIX_TWO = 1.0 - 0.95**10
BF = jnp.bfloat16
F32 = jnp.float32


def contract(left, right, left_dim, right_dim):
    return lax.dot_general(
        left, right, (((left_dim,), (right_dim,)), ((), ())), preferred_element_type=F32
    )


def to_tile(blocks):
    out = lax.all_to_all(blocks, "mp", split_axis=1, concat_axis=1, tiled=True)
    k, n, r, c = out.shape
    return out.transpose(0, 2, 1, 3).reshape(k, r, n * c)


def to_home(rows, n):
    k, r, c = rows.shape
    out = rows.reshape(k, r, n, c // n).transpose(0, 2, 1, 3)
    return lax.all_to_all(out, "mp", split_axis=1, concat_axis=1, tiled=True)


def gather_rows(rows):
    return lax.all_gather(rows, "dp", axis=0, tiled=True)


def normalize(power):
    wide = power.astype(F32)
    return lax.rsqrt(jnp.sum(wide * wide, axis=0, keepdims=True) + 1e-06)


def shards(
    features,
    out_grads,
    norm_grads,
    owners,
    moment1,
    moment2,
    left_stats,
    right_stats,
    left_basis,
    right_basis,
    norm_m,
    norm_v,
):
    dp = lax.axis_size("dp")
    tiles, slab, width = moment1.shape
    full = slab * dp
    me = lax.axis_index("dp")
    row0 = me * slab

    narrow = to_tile(jnp.stack([left_basis, right_basis, left_stats, right_stats]).astype(BF))
    left_full = gather_rows(narrow[0])
    right_full = gather_rows(narrow[1])

    flat = out_grads.reshape(out_grads.shape[0], tiles * width)
    partial = contract(features, flat, 0, 0).astype(BF).reshape(dp, slab, tiles * width)
    parts = lax.all_to_all(partial, "dp", split_axis=0, concat_axis=0, tiled=True)
    grad_home = jnp.sum(parts.astype(F32), axis=0).astype(BF)
    grad_home = grad_home.reshape(slab, tiles, width).transpose(1, 0, 2)
    grad_rows = to_tile(grad_home[None])[0]
    grad_full = gather_rows(grad_rows)

    wide = to_tile(jnp.stack([moment1, moment2]))

    prod_l = contract(grad_rows, grad_full, 1, 1)
    grad_cols = lax.dynamic_slice_in_dim(grad_full, row0, slab, 1)
    prod_r = contract(grad_cols, grad_full, 0, 0)
    stats_l = (0.95 * narrow[2].astype(F32) + 0.05 * prod_l).astype(BF)
    stats_r = (0.95 * narrow[3].astype(F32) + 0.05 * prod_r).astype(BF)
    power_l = contract(stats_l, left_full, 1, 0).astype(BF)
    power_r = contract(stats_r, right_full, 1, 0).astype(BF)
    power_l_full = gather_rows(power_l)
    power_r_full = gather_rows(power_r)

    left_cols = lax.dynamic_slice_in_dim(left_full, row0, slab, 1)
    half = contract(left_cols, grad_full, 0, 0).astype(BF)
    rotated = contract(half, right_full, 1, 0)
    tile_one = 0.9 * wide[0] + 0.1 * rotated
    tile_two = 0.95 * wide[1] + 0.05 * rotated * rotated
    direction = (tile_one / FIX_ONE / (jnp.sqrt(tile_two / FIX_TWO) + 1e-08)).astype(BF)
    back = contract(direction, right_full, 1, 1).astype(BF)
    back_full = gather_rows(back)

    home1 = to_home(jnp.stack([rotated, prod_l, prod_r]).astype(BF), tiles).astype(F32)
    new_one = 0.9 * moment1 + 0.1 * home1[0]
    new_two = 0.95 * moment2 + 0.05 * home1[0] * home1[0]
    new_sl = 0.95 * left_stats + 0.05 * home1[1]
    new_sr = 0.95 * right_stats + 0.05 * home1[2]

    update = contract(narrow[0], back_full, 1, 0).astype(BF)

    def refine(power_full, power_rows):
        scale = normalize(power_full)
        iter_full = (power_full.astype(F32) * scale).astype(BF)
        iter_rows = (power_rows.astype(F32) * scale).astype(BF)
        gram = contract(iter_rows, iter_full, 1, 1).astype(BF)
        return 1.5 * iter_rows.astype(F32) - 0.5 * contract(gram, iter_full, 1, 0)

    new_l = refine(power_l_full, power_l)
    new_r = refine(power_r_full, power_r)
    home2 = to_home(jnp.stack([new_l.astype(BF), new_r.astype(BF), update]), tiles)
    new_bl = home2[0].astype(F32)
    new_br = home2[1].astype(F32)
    slot_of = jnp.arange(dp, dtype=jnp.int32)[:, None, None]
    slots = jnp.zeros((dp, slab, width), BF)
    for n in range(tiles):
        slots = jnp.where(slot_of == owners[n], home2[2, n][None], slots)
    update_slot = lax.all_to_all(slots, "dp", split_axis=0, concat_axis=0, tiled=True)
    update_slot = update_slot.reshape(1, full, width)

    norm_parts = norm_grads.reshape(dp, norm_m.shape[0])
    norm_parts = lax.all_to_all(norm_parts, "dp", split_axis=0, concat_axis=0, tiled=True)
    norm_total = jnp.sum(norm_parts, axis=0)
    new_nm = 0.9 * norm_m + 0.1 * norm_total
    new_nv = 0.95 * norm_v + 0.05 * norm_total * norm_total
    norm_step = new_nm / FIX_ONE / (jnp.sqrt(new_nv / FIX_TWO) + 1e-08)
    to_owner = (jnp.arange(dp, dtype=jnp.int32) == owners[tiles])[:, None]
    norm_out = jnp.where(to_owner, norm_step[None], 0.0)
    norm_slot = lax.all_to_all(norm_out, "dp", split_axis=0, concat_axis=0, tiled=True)
    norm_slot = norm_slot.reshape(1, -1)
    return (
        new_one,
        new_two,
        new_sl,
        new_sr,
        new_bl,
        new_br,
        update_slot,
        new_nm,
        new_nv,
        norm_slot,
    )


def solution(mesh):
    in_specs = (
        P("dp", None),
        P("dp", None, "mp"),
        P("dp", None),
        P(),
        P(None, "dp", "mp"),
        P(None, "dp", "mp"),
        P(None, "dp", "mp"),
        P(None, "dp", "mp"),
        P(None, "dp", "mp"),
        P(None, "dp", "mp"),
        P("dp"),
        P("dp"),
    )
    out_specs = (
        P(None, "dp", "mp"),
        P(None, "dp", "mp"),
        P(None, "dp", "mp"),
        P(None, "dp", "mp"),
        P(None, "dp", "mp"),
        P(None, "dp", "mp"),
        P("dp", None, "mp"),
        P("dp"),
        P("dp"),
        P("dp", None),
    )
    return jax.shard_map(shards, mesh=mesh, in_specs=in_specs, out_specs=out_specs, check_vma=False)
```
